32 devices in a mesh: rep: 8 (over z, y), shard: 4 (over x, core).
Axes of the slice: x: 2, y: 2, z: 4, core: 2. Of those that a mesh axis runs over, the one named last changes fastest.
Arguments:
- tokens: bfloat16 [4096, 1024], P(('rep', 'shard')), may hold values from -6 to 6
- cotangent: bfloat16 [4096, 1024], P(('rep', 'shard')), may hold values from -6 to 6
- doc_ids: int32 [4096], P(('rep', 'shard')), may hold values from -1 to 15, as said below
- w_query: bfloat16 [1024, 1024], P('shard'), may hold values from -0.1875 to 0.1875
- w_key: bfloat16 [1024, 512], P('shard'), may hold values from -0.1875 to 0.1875
- w_value: bfloat16 [1024, 512], P('shard'), may hold values from -0.1875 to 0.1875
- w_out: bfloat16 [1024, 1024], P('shard'), may hold values from -0.5 to 0.5
- w_gate: bfloat16 [1024, 4608], P('shard'), may hold values from -0.1875 to 0.1875
- w_up: bfloat16 [1024, 4608], P('shard'), may hold values from -0.1875 to 0.1875
- w_down: bfloat16 [4608, 1024], P('shard'), may hold values from -0.09375 to 0.09375
- gain_attn: bfloat16 [1024], P('shard'), may hold values from 0.5 to 1.5
- gain_ffn: bfloat16 [1024], P('shard'), may hold values from 0.5 to 1.5
- gain_query: bfloat16 [64], P('shard'), may hold values from 0.5 to 1.5
- gain_key: bfloat16 [64], P('shard'), may hold values from 0.5 to 1.5
Outputs:
- block_out: bfloat16 [4096, 1024], P(('rep', 'shard'))
- grad_tokens: float32 [4096, 1024], P(('rep', 'shard'))
- grad_w_query: float32 [1024, 1024], P('shard')
- grad_w_key: float32 [1024, 512], P('shard')
- grad_w_value: float32 [1024, 512], P('shard')
- grad_w_out: float32 [1024, 1024], P('shard')
- grad_w_gate: float32 [1024, 4608], P('shard')
- grad_w_up: float32 [1024, 4608], P('shard')
- grad_w_down: float32 [4608, 1024], P('shard')
- grad_gain_attn: float32 [1024], P('shard')
- grad_gain_ffn: float32 [1024], P('shard')
- grad_gain_query: float32 [64], P('shard')
- grad_gain_key: float32 [64], P('shard')
The draws below stay inside these ranges and needn't reach their ends.
Inputs may be any that keep to these rules, and one draw needn't show every extreme that they name: `doc_ids`: each device's 128 slots hold its sequences one after another, numbered from 0 upward without gaps, followed by its empty slots marked -1; at least one device has no empty slot and holds 16 sequences.
All inputs are finite; a program needn't handle non-finite values.
Results may differ from the reference program's by a relative error of at most 0.02.
Values may be sent and summed in bfloat16 or wider, within the bound.
A program may use at most 192 MiB of HBM per device.

```python
import math
import jax
import jax.numpy as jnp
from jax import lax

D = 1024
QH = 16
KVH = 8
HEAD_DIM = 64
FF = 4608
TOK_DEV = 128
QW = 1024
KW = 512
TOKENS = 4096
N_REP = 8
N_SHARD = 4


def draw_doc_ids(key, part):
    dev_count = TOKENS // TOK_DEV
    top_seq = TOK_DEV // 8 - 1
    key_live, key_full, key_cuts = jax.random.split(key, 3)
    live_count = jax.random.randint(key_live, (dev_count,), TOK_DEV // 4, TOK_DEV)
    full_device = jax.random.randint(key_full, (), 0, dev_count)
    is_full = jnp.arange(dev_count) == full_device
    live_count = jnp.where(is_full, TOK_DEV, live_count)
    cut_marks = (jax.random.randint(key_cuts, (dev_count, TOK_DEV), 0, 32) == 0).astype(jnp.int32)
    slot_index = jnp.arange(TOK_DEV)[None, :]
    even_cuts = (slot_index % 8 == 0).astype(jnp.int32)
    cut_marks = jnp.where(is_full[:, None], even_cuts, cut_marks)
    cut_marks = cut_marks.at[:, 0].set(0)
    seq_index = jnp.minimum(jnp.cumsum(cut_marks, axis=1), top_seq)
    seq_index = jnp.where(slot_index < live_count[:, None], seq_index, -1)
    return seq_index.reshape(-1).astype(jnp.int32)


def shard_levels(key, dims, cuts, least, high):
    factor_of = 1.0
    for dim, blocks in cuts:
        steps = jax.random.uniform(jax.random.fold_in(jax.random.fold_in(key, 6), dim), (blocks,), jnp.float32, least / len(cuts), high / len(cuts))
        factor_of = factor_of * jnp.repeat(jnp.exp(steps), dims[dim] // blocks).reshape((-1,) + (1,) * (len(dims) - 1 - dim))
    return factor_of


def noise(key, dims, scale, limit, cuts=(), kind=jnp.bfloat16):
    loudness = shard_levels(key, dims, cuts, -0.22, 0.18) if cuts else 1.0
    values = jax.random.normal(key, dims, jnp.float32) * scale * loudness
    return jnp.minimum(jnp.maximum(values, -limit), limit).astype(kind)


def setup_inputs(seed: int = 0) -> dict:
    key_list = jax.random.split(jax.random.key(seed), 15)
    tokens = noise(key_list[0], (TOKENS, D), 1.0, 6.0, ((0, 32),))
    cotangent = noise(key_list[1], (TOKENS, D), 1.0, 6.0, ((0, 32),))
    doc_ids = draw_doc_ids(jax.random.fold_in(key_list[14], 71), 0)
    w_query = noise(key_list[3], (D, QW), D ** -0.5, 0.1875, ((0, 4),))
    w_key = noise(key_list[4], (D, KW), D ** -0.5, 0.1875, ((0, 4),))
    w_value = noise(key_list[5], (D, KW), D ** -0.5, 0.1875, ((0, 4),))
    w_out = noise(key_list[6], (QW, D), (QW // 8) ** -0.5, 0.5, ((0, 4),))
    w_gate = noise(key_list[7], (D, FF), D ** -0.5, 0.1875, ((0, 4),))
    w_up = noise(key_list[8], (D, FF), D ** -0.5, 0.1875, ((0, 4),))
    w_down = noise(key_list[9], (FF, D), FF ** -0.5, 0.09375, ((0, 4),))
    gain_attn = jnp.clip(1.0 + 0.1 * jax.random.normal(key_list[10], (D,), jnp.float32), 0.5, 1.5).astype(jnp.bfloat16)
    gain_ffn = jnp.clip(1.0 + 0.1 * jax.random.normal(key_list[11], (D,), jnp.float32), 0.5, 1.5).astype(jnp.bfloat16)
    gain_query = jnp.clip(1.0 + 0.1 * jax.random.normal(key_list[12], (HEAD_DIM,), jnp.float32), 0.5, 1.5).astype(jnp.bfloat16)
    gain_key = jnp.clip(1.0 + 0.1 * jax.random.normal(key_list[13], (HEAD_DIM,), jnp.float32), 0.5, 1.5).astype(jnp.bfloat16)
    return {"tokens": tokens, "cotangent": cotangent, "doc_ids": doc_ids, "w_query": w_query, "w_key": w_key, "w_value": w_value, "w_out": w_out, "w_gate": w_gate, "w_up": w_up, "w_down": w_down, "gain_attn": gain_attn, "gain_ffn": gain_ffn, "gain_query": gain_query, "gain_key": gain_key}


NORM_EPSILON = 1e-05
ROPE_BASE = 1000000.0

def matmul(left, right):
    return jnp.dot(left, right, preferred_element_type=jnp.float32)

def norm_rows(values, gain_vec):
    inv_rms = lax.rsqrt(lax.optimization_barrier(jnp.mean(values * values, axis=-1, keepdims=True)) + NORM_EPSILON)
    normed = values * inv_rms
    return (normed * gain_vec.astype(jnp.float32), normed, inv_rms)

def norm_back(grad_out, normed, inv_rms, gain_vec):
    scaled = grad_out * gain_vec.astype(jnp.float32)
    grad_in = inv_rms * (scaled - normed * lax.optimization_barrier(jnp.mean(scaled * normed, axis=-1, keepdims=True)))
    return grad_in

def round_total(batched):
    rounded = lax.optimization_barrier(batched.astype(jnp.bfloat16))
    return lax.optimization_barrier(jnp.sum(rounded.astype(jnp.float32), axis=0))

def device_product(left, right, dev_group):
    left_dev = left.reshape(dev_group, -1, left.shape[-1]).astype(jnp.float32)
    right_dev = right.reshape(dev_group, -1, right.shape[-1]).astype(jnp.float32)
    return round_total(jnp.einsum('gta,gtb->gab', left_dev, right_dev))

def device_gain(grad_out, normed, dev_group):
    product = (grad_out * normed).reshape(dev_group, -1, grad_out.shape[-1])
    return round_total(lax.optimization_barrier(jnp.sum(product, axis=1)))

def doc_tables(doc_rows):
    block_len = doc_rows.shape[-1]
    row_index = jnp.arange(block_len)[:, None]
    col_index = jnp.arange(block_len)[None, :]
    same_doc = doc_rows[:, :, None] == doc_rows[:, None, :]
    allowed = same_doc & (row_index >= col_index)[None]
    earlier = same_doc & (row_index > col_index)[None]
    positions = lax.optimization_barrier(jnp.sum(earlier.astype(jnp.int32), axis=2))
    return (allowed, positions)

def rope_tables(positions, head_dim):
    half_dim = head_dim // 2
    inv_freq = jnp.exp(jnp.arange(half_dim).astype(jnp.float32) * (-2.0 * math.log(ROPE_BASE) / head_dim))
    angles = positions.astype(jnp.float32)[:, :, None, None] * inv_freq
    return (jnp.cos(angles), jnp.sin(angles))

def rotate(values, cos_tab, sin_tab):
    half_dim = values.shape[-1] // 2
    part_one = values[..., :half_dim]
    part_two = values[..., half_dim:]
    return jnp.concatenate([part_one * cos_tab - part_two * sin_tab, part_two * cos_tab + part_one * sin_tab], axis=-1)

def rotate_back(values, cos_tab, sin_tab):
    half_dim = values.shape[-1] // 2
    part_one = values[..., :half_dim]
    part_two = values[..., half_dim:]
    return jnp.concatenate([part_one * cos_tab + part_two * sin_tab, part_two * cos_tab - part_one * sin_tab], axis=-1)

def reference(tokens, cotangent, doc_ids, w_query, w_key, w_value, w_out, w_gate, w_up, w_down, gain_attn, gain_ffn, gain_query, gain_key):
    devices = N_REP * N_SHARD
    dev_group = math.gcd(devices, max(1, 1024 // TOK_DEV))
    blocks = devices // dev_group
    block_rows = dev_group * TOK_DEV
    head_share = QH // KVH
    score_scale = 1.0 / math.sqrt(HEAD_DIM)

    def block_step(totals, pieces):
        block_tokens, block_cot, doc_rows = pieces
        allowed, positions = doc_tables(doc_rows)
        key_mask = allowed[:, None, None]
        cos_tab, sin_tab = rope_tables(positions, HEAD_DIM)
        resid_in = block_tokens.astype(jnp.float32)
        normed_in, unit_in, rms_in = norm_rows(resid_in, gain_attn)
        normed_bf = normed_in.astype(jnp.bfloat16)
        query_raw = matmul(normed_bf, w_query).reshape(dev_group, TOK_DEV, QH, HEAD_DIM)
        key_raw = matmul(normed_bf, w_key).reshape(dev_group, TOK_DEV, KVH, HEAD_DIM)
        value_bf = matmul(normed_bf, w_value).astype(jnp.bfloat16).reshape(dev_group, TOK_DEV, KVH, HEAD_DIM)
        query_normed, query_unit, query_rms = norm_rows(query_raw, gain_query)
        key_normed, key_unit, key_rms = norm_rows(key_raw, gain_key)
        query_bf = rotate(query_normed, cos_tab, sin_tab).astype(jnp.bfloat16).reshape(dev_group, TOK_DEV, KVH, head_share, HEAD_DIM)
        key_bf = rotate(key_normed, cos_tab, sin_tab).astype(jnp.bfloat16)
        scores = jnp.einsum('gqkrd,gskd->gkrqs', query_bf.astype(jnp.float32), key_bf.astype(jnp.float32)) * score_scale
        log_total = jnp.log(lax.optimization_barrier(jnp.sum(jnp.where(key_mask, jnp.exp(scores), 0.0), axis=-1, keepdims=True)))
        attn_probs = jnp.where(key_mask, jnp.exp(scores - log_total), 0.0)
        probs_bf = attn_probs.astype(jnp.bfloat16)
        mixed_bf = jnp.einsum('gkrqs,gskd->gqkrd', probs_bf.astype(jnp.float32), value_bf.astype(jnp.float32)).astype(jnp.bfloat16).reshape(block_rows, QH * HEAD_DIM)
        resid_mid = resid_in + matmul(mixed_bf, w_out)
        normed_mid, unit_mid, rms_mid = norm_rows(resid_mid, gain_ffn)
        hidden_in = normed_mid.astype(jnp.bfloat16)
        gate_proj = matmul(hidden_in, w_gate)
        up_proj = matmul(hidden_in, w_up)
        gate_sig = jax.nn.sigmoid(gate_proj)
        gate_act = gate_proj * gate_sig
        hidden_bf = (gate_act * up_proj).astype(jnp.bfloat16)
        block_out = (resid_mid + matmul(hidden_bf, w_down)).astype(jnp.bfloat16)
        live_rows = (doc_rows.reshape(block_rows) >= 0).astype(jnp.float32)[:, None]
        grad_y = block_cot.astype(jnp.float32) * live_rows
        grad_y_bf = grad_y.astype(jnp.bfloat16)
        part_down = device_product(hidden_bf, grad_y_bf, dev_group)
        grad_hidden = matmul(grad_y_bf, w_down.T)
        grad_gate_bf = (grad_hidden * up_proj * gate_sig * (1.0 + gate_proj * (1.0 - gate_sig))).astype(jnp.bfloat16)
        grad_up_bf = (grad_hidden * gate_act).astype(jnp.bfloat16)
        part_gate = device_product(hidden_in, grad_gate_bf, dev_group)
        part_up = device_product(hidden_in, grad_up_bf, dev_group)
        grad_norm_mid = matmul(grad_gate_bf, w_gate.T) + matmul(grad_up_bf, w_up.T)
        back_mid = norm_back(grad_norm_mid, unit_mid, rms_mid, gain_ffn)
        part_gffn = device_gain(grad_norm_mid, unit_mid, dev_group)
        grad_mid = grad_y + back_mid
        grad_mid_bf = grad_mid.astype(jnp.bfloat16)
        part_out = device_product(mixed_bf, grad_mid_bf, dev_group)
        grad_mixed_bf = matmul(grad_mid_bf, w_out.T).astype(jnp.bfloat16).reshape(dev_group, TOK_DEV, KVH, head_share, HEAD_DIM)
        grad_scores = jnp.einsum('gqkrd,gskd->gkrqs', grad_mixed_bf.astype(jnp.float32), value_bf.astype(jnp.float32))
        grad_value_bf = jnp.einsum('gkrqs,gqkrd->gskd', probs_bf.astype(jnp.float32), grad_mixed_bf.astype(jnp.float32)).astype(jnp.bfloat16).reshape(block_rows, KVH * HEAD_DIM)
        row_dot = lax.optimization_barrier(jnp.sum(attn_probs * grad_scores, axis=-1, keepdims=True))
        grad_logits = (attn_probs * (grad_scores - row_dot) * score_scale).astype(jnp.bfloat16)
        grad_query_rot = jnp.einsum('gkrqs,gskd->gqkrd', grad_logits.astype(jnp.float32), key_bf.astype(jnp.float32)).reshape(dev_group, TOK_DEV, QH, HEAD_DIM)
        grad_key_rot = jnp.einsum('gkrqs,gqkrd->gskd', grad_logits.astype(jnp.float32), query_bf.astype(jnp.float32))
        query_back = rotate_back(grad_query_rot, cos_tab, sin_tab)
        key_back = rotate_back(grad_key_rot, cos_tab, sin_tab)
        grad_query_raw = norm_back(query_back, query_unit, query_rms, gain_query)
        grad_key_raw = norm_back(key_back, key_unit, key_rms, gain_key)
        part_gquery = device_gain(query_back, query_unit, dev_group)
        part_gkey = device_gain(key_back, key_unit, dev_group)
        grad_query_bf = grad_query_raw.astype(jnp.bfloat16).reshape(block_rows, QH * HEAD_DIM)
        grad_key_bf = grad_key_raw.astype(jnp.bfloat16).reshape(block_rows, KVH * HEAD_DIM)
        part_query = device_product(normed_bf, grad_query_bf, dev_group)
        part_key = device_product(normed_bf, grad_key_bf, dev_group)
        part_value = device_product(normed_bf, grad_value_bf, dev_group)
        grad_norm_in = matmul(grad_query_bf, w_query.T) + matmul(grad_key_bf, w_key.T) + matmul(grad_value_bf, w_value.T)
        back_in = norm_back(grad_norm_in, unit_in, rms_in, gain_attn)
        part_gattn = device_gain(grad_norm_in, unit_in, dev_group)
        grad_input = grad_mid + back_in
        parts = (part_query, part_key, part_value, part_out, part_gate, part_up, part_down, part_gattn, part_gffn, part_gquery, part_gkey)
        totals = tuple((total_one + part_one for total_one, part_one in zip(totals, parts)))
        return (totals, (block_out, grad_input))
    shapes = [w_query.shape, w_key.shape, w_value.shape, w_out.shape, w_gate.shape, w_up.shape, w_down.shape, gain_attn.shape, gain_ffn.shape, gain_query.shape, gain_key.shape]
    start = tuple((jnp.zeros(shape_one, jnp.float32) for shape_one in shapes))
    inputs = (tokens.reshape(blocks, block_rows, D), cotangent.reshape(blocks, block_rows, D), doc_ids.reshape(blocks, dev_group, TOK_DEV))
    totals, stacked = lax.scan(block_step, start, inputs)
    block_out = stacked[0].reshape(TOKENS, D)
    grad_tokens = stacked[1].reshape(TOKENS, D)
    return (block_out, grad_tokens, totals[0], totals[1], totals[2], totals[3], totals[4], totals[5], totals[6], totals[7], totals[8], totals[9], totals[10])
```

```python
import functools
import math

import jax
import jax.numpy as jnp
from jax import lax
from jax.sharding import PartitionSpec as P

QH = 16
KVH = 8
HEAD_DIM = 64


NORM_EPSILON = 1e-05
ROPE_BASE = 1000000.0


def matmul(left, right):
    return jnp.dot(left, right, preferred_element_type=jnp.float32)


def norm_rows(values, gain_vec):
    inv_rms = lax.rsqrt(jnp.mean(values * values, axis=-1, keepdims=True) + NORM_EPSILON)
    normed = values * inv_rms
    return (normed * gain_vec.astype(jnp.float32), normed, inv_rms)


def norm_back(grad_out, normed, inv_rms, gain_vec):
    scaled = grad_out * gain_vec.astype(jnp.float32)
    grad_in = inv_rms * (scaled - normed * jnp.mean(scaled * normed, axis=-1, keepdims=True))
    lead_axes = tuple(range(grad_out.ndim - 1))
    return (grad_in, jnp.sum(grad_out * normed, axis=lead_axes))


def doc_tables(doc_rows):
    block_len = doc_rows.shape[-1]
    row_index = jnp.arange(block_len)[:, None]
    col_index = jnp.arange(block_len)[None, :]
    same_doc = doc_rows[:, :, None] == doc_rows[:, None, :]
    allowed = same_doc & (row_index >= col_index)[None]
    earlier = same_doc & (row_index > col_index)[None]
    positions = jnp.sum(earlier.astype(jnp.int32), axis=2)
    return (allowed, positions)


def rope_tables(positions, head_dim):
    half_dim = head_dim // 2
    inv_freq = jnp.exp(
        jnp.arange(half_dim).astype(jnp.float32) * (-2.0 * math.log(ROPE_BASE) / head_dim)
    )
    angles = positions.astype(jnp.float32)[:, :, None, None] * inv_freq
    return (jnp.cos(angles), jnp.sin(angles))


def rotate(values, cos_tab, sin_tab):
    half_dim = values.shape[-1] // 2
    part_one = values[..., :half_dim]
    part_two = values[..., half_dim:]
    return jnp.concatenate(
        [part_one * cos_tab - part_two * sin_tab, part_two * cos_tab + part_one * sin_tab], axis=-1
    )


def rotate_back(values, cos_tab, sin_tab):
    half_dim = values.shape[-1] // 2
    part_one = values[..., :half_dim]
    part_two = values[..., half_dim:]
    return jnp.concatenate(
        [part_one * cos_tab + part_two * sin_tab, part_two * cos_tab - part_one * sin_tab], axis=-1
    )


def attn_probs_of(query_bf, key_bf, key_mask, log_total, score_scale):
    scores = (
        jnp.einsum("gqkrd,gskd->gkrqs", query_bf, key_bf, preferred_element_type=jnp.float32)
        * score_scale
    )
    if log_total is None:
        log_total = jnp.log(
            jnp.sum(jnp.where(key_mask, jnp.exp(scores), 0.0), axis=-1, keepdims=True)
        )
    return (jnp.where(key_mask, jnp.exp(scores - log_total), 0.0), log_total)


def bit_count(size):
    return size.bit_length() - 1


def swap(values, axis_name, axis_size, bit):
    return lax.ppermute(values, axis_name, [(i, i ^ (1 << bit)) for i in range(axis_size)])


def gather_pieces(weight, n_shard, n_rep):
    rows = weight.shape[0]
    me = lax.axis_index("shard")
    pieces = [(me * rows, weight)]
    far = []
    if n_rep > 1 and rows % 2 == 0:
        half = rows // 2
        lane = lax.axis_index("rep") & 1
        mine = [(0, lax.dynamic_slice_in_dim(weight, lane * half, half, axis=0))]
        for bit in reversed(range(1, bit_count(n_shard))):
            mine = mine + [(j ^ (1 << bit), swap(w, "shard", n_shard, bit)) for j, w in mine]
        for j, w in mine[1:]:
            far.append(((me ^ j) * rows + lane * half, j, lane * half, w))
            far.append(((me ^ j) * rows + (1 - lane) * half, j, (1 - lane) * half, swap(w, "rep", n_rep, 0)))
    else:
        mine = [(0, weight)]
        for bit in reversed(range(1, bit_count(n_shard))):
            mine = mine + [(j ^ (1 << bit), swap(w, "shard", n_shard, bit)) for j, w in mine]
        for j, w in mine[1:]:
            far.append(((me ^ j) * rows, j, 0, w))
    if n_shard > 1:
        pieces.append(((me ^ 1) * rows, swap(weight, "shard", n_shard, 0)))
    for start, j, inner, w in far:
        pieces.append((start, w))
        pieces.append(((me ^ j ^ 1) * rows + inner, swap(w, "shard", n_shard, 0)))
    return pieces


def times(left, pieces):
    total = None
    for start, w in pieces:
        part = matmul(lax.dynamic_slice_in_dim(left, start, w.shape[0], axis=1), w)
        total = part if total is None else total + part
    return total


def times_t(left, pieces, depth):
    total = jnp.zeros((left.shape[0], depth), jnp.float32)
    for start, w in pieces:
        part = lax.dot_general(left, w, (((1,), (1,)), ((), ())), preferred_element_type=jnp.float32)
        total = lax.dynamic_update_slice_in_dim(total, part, start, axis=1)
    return total


def relative_rows(left, n_shard, n_rep):
    tok, depth = left.shape
    s_bits, r_bits = bit_count(n_shard), bit_count(n_rep)
    rows = depth // (n_shard * n_rep)
    blocks = left.T.reshape((2,) * (s_bits + r_bits) + (rows, tok))
    order = tuple(reversed(range(s_bits))) + tuple(reversed(range(s_bits, s_bits + r_bits)))
    blocks = blocks.transpose(order + (s_bits + r_bits, s_bits + r_bits + 1))
    me, rep = lax.axis_index("shard"), lax.axis_index("rep")
    for i in range(s_bits + r_bits):
        on = ((me >> i) & 1) if i < s_bits else ((rep >> (i - s_bits)) & 1)
        blocks = jnp.where(on == 1, jnp.flip(blocks, axis=i), blocks)
    return blocks


def grad_of(blocks, right, n_shard, n_rep):
    s_bits, r_bits = bit_count(n_shard), bit_count(n_rep)
    cols = right.shape[1]

    def part(rows_of):
        return matmul(rows_of.reshape(-1, rows_of.shape[-1]), right).astype(jnp.bfloat16)

    steps = [("shard", n_shard, i) for i in range(s_bits)] + [("rep", n_rep, i) for i in range(r_bits)]
    if not steps:
        return part(blocks).astype(jnp.float32)
    send, keep = part(blocks[1]), part(blocks[0])
    for k, (name, size, bit) in enumerate(steps):
        got = swap(send, name, size, bit)
        total = (keep.astype(jnp.float32) + got.astype(jnp.float32)).astype(jnp.bfloat16)
        if k + 1 < len(steps):
            half = total.shape[0] // 2
            keep, send = total[:half], total[half:]
    return lax.all_gather(total, "rep", axis=0, tiled=True).astype(jnp.float32)


def local(
    n_rep,
    n_shard,
    tokens,
    cotangent,
    doc_ids,
    w_query,
    w_key,
    w_value,
    w_out,
    w_gate,
    w_up,
    w_down,
    gain_attn,
    gain_ffn,
    gain_query,
    gain_key,
):
    tok_rows, width = tokens.shape
    ff = w_gate.shape[1]
    q_width, k_width = w_query.shape[1], w_key.shape[1]
    head_share = QH // KVH
    score_scale = 1.0 / math.sqrt(HEAD_DIM)
    gains = (gain_attn, gain_ffn, gain_query, gain_key)
    gain_sizes = [g.shape[0] for g in gains]
    gain_ends = [sum(gain_sizes[: i + 1]) for i in range(len(gains))]
    all_gains = lax.all_gather(jnp.concatenate(gains), "shard", axis=0)
    full_gattn, full_gffn, full_gquery, full_gkey = (
        all_gains[:, end - size : end].reshape(-1) for size, end in zip(gain_sizes, gain_ends)
    )
    qkv_set = gather_pieces(jnp.concatenate([w_query, w_key, w_value], axis=1), n_shard, n_rep)
    out_set = gather_pieces(w_out, n_shard, n_rep)
    gate_set = gather_pieces(w_gate, n_shard, n_rep)
    up_set = gather_pieces(w_up, n_shard, n_rep)
    down_set = gather_pieces(w_down, n_shard, n_rep)

    doc_rows = doc_ids[None, :]
    allowed, positions = doc_tables(doc_rows)
    key_mask = allowed[:, None, None]
    cos_tab, sin_tab = rope_tables(positions, HEAD_DIM)
    resid_in = tokens.astype(jnp.float32)
    normed_in, unit_in, rms_in = norm_rows(resid_in, full_gattn)
    normed_bf = normed_in.astype(jnp.bfloat16)
    qkv = times(normed_bf, qkv_set)
    query_raw = qkv[:, :q_width].reshape(1, tok_rows, QH, HEAD_DIM)
    key_raw = qkv[:, q_width : q_width + k_width].reshape(1, tok_rows, KVH, HEAD_DIM)
    value_bf = qkv[:, q_width + k_width :].astype(jnp.bfloat16).reshape(1, tok_rows, KVH, HEAD_DIM)
    query_normed, query_unit, query_rms = norm_rows(query_raw, full_gquery)
    key_normed, key_unit, key_rms = norm_rows(key_raw, full_gkey)
    query_bf = (
        rotate(query_normed, cos_tab, sin_tab)
        .astype(jnp.bfloat16)
        .reshape(1, tok_rows, KVH, head_share, HEAD_DIM)
    )
    key_bf = rotate(key_normed, cos_tab, sin_tab).astype(jnp.bfloat16)
    attn_probs, log_total = attn_probs_of(query_bf, key_bf, key_mask, None, score_scale)
    probs_bf = attn_probs.astype(jnp.bfloat16)
    mixed_bf = (
        jnp.einsum("gkrqs,gskd->gqkrd", probs_bf, value_bf, preferred_element_type=jnp.float32)
        .astype(jnp.bfloat16)
        .reshape(tok_rows, QH * HEAD_DIM)
    )
    resid_mid = resid_in + times(mixed_bf, out_set)
    normed_mid, unit_mid, rms_mid = norm_rows(resid_mid, full_gffn)
    hidden_in = normed_mid.astype(jnp.bfloat16)
    gate_proj = times(hidden_in, gate_set)
    up_proj = times(hidden_in, up_set)
    gate_sig = jax.nn.sigmoid(gate_proj)
    gate_act = gate_proj * gate_sig
    hidden_bf = (gate_act * up_proj).astype(jnp.bfloat16)

    live_rows = (doc_ids >= 0).astype(jnp.float32)[:, None]
    grad_y = cotangent.astype(jnp.float32) * live_rows
    grad_y_bf = grad_y.astype(jnp.bfloat16)
    grad_down = grad_of(relative_rows(hidden_bf, n_shard, n_rep), grad_y_bf, n_shard, n_rep)
    block_out = (resid_mid + times(hidden_bf, down_set)).astype(jnp.bfloat16)

    grad_hidden = times_t(grad_y_bf, down_set, ff)
    grad_gate_bf = (grad_hidden * up_proj * gate_sig * (1.0 + gate_proj * (1.0 - gate_sig))).astype(
        jnp.bfloat16
    )
    grad_up_bf = (grad_hidden * gate_act).astype(jnp.bfloat16)
    mid_rows = relative_rows(hidden_in, n_shard, n_rep)
    grad_gate = grad_of(mid_rows, grad_gate_bf, n_shard, n_rep)
    grad_up = grad_of(mid_rows, grad_up_bf, n_shard, n_rep)
    grad_norm_mid = times_t(grad_gate_bf, gate_set, width) + times_t(grad_up_bf, up_set, width)
    back_mid, part_gffn = norm_back(grad_norm_mid, unit_mid, rms_mid, full_gffn)
    grad_mid = grad_y + back_mid
    grad_mid_bf = grad_mid.astype(jnp.bfloat16)
    grad_out = grad_of(relative_rows(mixed_bf, n_shard, n_rep), grad_mid_bf, n_shard, n_rep)
    grad_mixed_bf = (
        times_t(grad_mid_bf, out_set, q_width)
        .astype(jnp.bfloat16)
        .reshape(1, tok_rows, KVH, head_share, HEAD_DIM)
    )
    grad_scores = jnp.einsum(
        "gqkrd,gskd->gkrqs", grad_mixed_bf, value_bf, preferred_element_type=jnp.float32
    )
    grad_value_bf = (
        jnp.einsum("gkrqs,gqkrd->gskd", probs_bf, grad_mixed_bf, preferred_element_type=jnp.float32)
        .astype(jnp.bfloat16)
        .reshape(tok_rows, KVH * HEAD_DIM)
    )
    row_dot = jnp.sum(attn_probs * grad_scores, axis=-1, keepdims=True)
    grad_logits = (attn_probs * (grad_scores - row_dot) * score_scale).astype(jnp.bfloat16)
    grad_query_rot = jnp.einsum(
        "gkrqs,gskd->gqkrd", grad_logits, key_bf, preferred_element_type=jnp.float32
    ).reshape(1, tok_rows, QH, HEAD_DIM)
    grad_key_rot = jnp.einsum(
        "gkrqs,gqkrd->gskd", grad_logits, query_bf, preferred_element_type=jnp.float32
    )
    grad_query_raw, part_gquery = norm_back(
        rotate_back(grad_query_rot, cos_tab, sin_tab), query_unit, query_rms, full_gquery
    )
    grad_key_raw, part_gkey = norm_back(
        rotate_back(grad_key_rot, cos_tab, sin_tab), key_unit, key_rms, full_gkey
    )
    grad_query_bf = grad_query_raw.astype(jnp.bfloat16).reshape(tok_rows, QH * HEAD_DIM)
    grad_key_bf = grad_key_raw.astype(jnp.bfloat16).reshape(tok_rows, KVH * HEAD_DIM)
    grad_qkv_bf = jnp.concatenate([grad_query_bf, grad_key_bf, grad_value_bf], axis=1)
    grad_qkv = grad_of(relative_rows(normed_bf, n_shard, n_rep), grad_qkv_bf, n_shard, n_rep)
    grad_query = grad_qkv[:, :q_width]
    grad_key = grad_qkv[:, q_width : q_width + k_width]
    grad_value = grad_qkv[:, q_width + k_width :]
    grad_norm_in = times_t(grad_qkv_bf, qkv_set, width)
    back_in, part_gattn = norm_back(grad_norm_in, unit_in, rms_in, full_gattn)
    grad_tokens = grad_mid + back_in
    part_gains = jnp.concatenate(
        [
            p.reshape(n_shard, -1)
            for p in (part_gattn, part_gffn, part_gquery, part_gkey)
        ],
        axis=1,
    )
    part_gains = part_gains.astype(jnp.bfloat16).astype(jnp.float32)
    sum_gains = lax.psum(part_gains, ("rep", "shard"))
    own_gains = lax.dynamic_index_in_dim(sum_gains, lax.axis_index("shard"), axis=0, keepdims=False)
    grad_gattn, grad_gffn, grad_gquery, grad_gkey = (
        own_gains[end - size : end] for size, end in zip(gain_sizes, gain_ends)
    )
    return (
        block_out,
        grad_tokens,
        grad_query,
        grad_key,
        grad_value,
        grad_out,
        grad_gate,
        grad_up,
        grad_down,
        grad_gattn,
        grad_gffn,
        grad_gquery,
        grad_gkey,
    )


def solution(mesh):
    return jax.shard_map(
        functools.partial(local, mesh.shape["rep"], mesh.shape["shard"]),
        mesh=mesh,
        in_specs=(
            P(("rep", "shard"), None),
            P(("rep", "shard"), None),
            P(("rep", "shard")),
            P("shard", None),
            P("shard", None),
            P("shard", None),
            P("shard", None),
            P("shard", None),
            P("shard", None),
            P("shard", None),
            P("shard"),
            P("shard"),
            P("shard"),
            P("shard"),
        ),
        out_specs=(
            P(("rep", "shard"), None),
            P(("rep", "shard"), None),
            P("shard", None),
            P("shard", None),
            P("shard", None),
            P("shard", None),
            P("shard", None),
            P("shard", None),
            P("shard", None),
            P("shard"),
            P("shard"),
            P("shard"),
            P("shard"),
        ),
        check_vma=False,
    )
```

```python
import functools
import math

import jax
import jax.numpy as jnp
from jax import lax
from jax.sharding import PartitionSpec as P

QH = 16
KVH = 8
HEAD_DIM = 64


NORM_EPSILON = 1e-05
ROPE_BASE = 1000000.0


def matmul(left, right):
    return jnp.dot(left, right, preferred_element_type=jnp.float32)


def norm_rows(values, gain_vec):
    inv_rms = lax.rsqrt(jnp.mean(values * values, axis=-1, keepdims=True) + NORM_EPSILON)
    normed = values * inv_rms
    return (normed * gain_vec.astype(jnp.float32), normed, inv_rms)


def norm_back(grad_out, normed, inv_rms, gain_vec):
    scaled = grad_out * gain_vec.astype(jnp.float32)
    grad_in = inv_rms * (scaled - normed * jnp.mean(scaled * normed, axis=-1, keepdims=True))
    lead_axes = tuple(range(grad_out.ndim - 1))
    return (grad_in, jnp.sum(grad_out * normed, axis=lead_axes))


def doc_tables(doc_rows):
    block_len = doc_rows.shape[-1]
    row_index = jnp.arange(block_len)[:, None]
    col_index = jnp.arange(block_len)[None, :]
    same_doc = doc_rows[:, :, None] == doc_rows[:, None, :]
    allowed = same_doc & (row_index >= col_index)[None]
    earlier = same_doc & (row_index > col_index)[None]
    positions = jnp.sum(earlier.astype(jnp.int32), axis=2)
    return (allowed, positions)


def rope_tables(positions, head_dim):
    half_dim = head_dim // 2
    inv_freq = jnp.exp(
        jnp.arange(half_dim).astype(jnp.float32) * (-2.0 * math.log(ROPE_BASE) / head_dim)
    )
    angles = positions.astype(jnp.float32)[:, :, None, None] * inv_freq
    return (jnp.cos(angles), jnp.sin(angles))


def rotate(values, cos_tab, sin_tab):
    half_dim = values.shape[-1] // 2
    part_one = values[..., :half_dim]
    part_two = values[..., half_dim:]
    return jnp.concatenate(
        [part_one * cos_tab - part_two * sin_tab, part_two * cos_tab + part_one * sin_tab], axis=-1
    )


def rotate_back(values, cos_tab, sin_tab):
    half_dim = values.shape[-1] // 2
    part_one = values[..., :half_dim]
    part_two = values[..., half_dim:]
    return jnp.concatenate(
        [part_one * cos_tab + part_two * sin_tab, part_two * cos_tab - part_one * sin_tab], axis=-1
    )


def attn_probs_of(query_bf, key_bf, key_mask, log_total, score_scale):
    scores = (
        jnp.einsum("gqkrd,gskd->gkrqs", query_bf, key_bf, preferred_element_type=jnp.float32)
        * score_scale
    )
    if log_total is None:
        log_total = jnp.log(
            jnp.sum(jnp.where(key_mask, jnp.exp(scores), 0.0), axis=-1, keepdims=True)
        )
    return (jnp.where(key_mask, jnp.exp(scores - log_total), 0.0), log_total)


def bit_count(size):
    return size.bit_length() - 1


def swap(values, axis_name, axis_size, bit):
    return lax.ppermute(values, axis_name, [(i, i ^ (1 << bit)) for i in range(axis_size)])


def after(values, earlier):
    if earlier is None:
        return values
    return lax.optimization_barrier((values, earlier))[0]


def gather_small(values, n_shard):
    rows = [values] + [
        lax.ppermute(values, "shard", [(i, i ^ j) for i in range(n_shard)]) for j in range(1, n_shard)
    ]
    got = jnp.stack(rows)
    me = lax.axis_index("shard")
    for bit in range(bit_count(n_shard)):
        pairs = got.reshape(-1, 2, 1 << bit, got.shape[-1])
        got = jnp.where((me >> bit) & 1 == 1, jnp.flip(pairs, axis=1), pairs).reshape(got.shape)
    return got


def gather_pieces(weight, n_shard, n_rep, earlier):
    rows = weight.shape[0]
    me = lax.axis_index("shard")
    split = n_rep > 1 and rows % 2 == 0
    first = weight
    if split:
        half = rows // 2
        lane = lax.axis_index("rep") & 1
        first = lax.dynamic_slice_in_dim(weight, lane * half, half, axis=0)
    mine = [(0, first)]
    for bit in reversed(range(1, bit_count(n_shard))):
        sent = [(j, after(w, earlier)) for j, w in mine]
        got = [(j ^ (1 << bit), swap(w, "shard", n_shard, bit)) for j, w in sent]
        mine, earlier = mine + got, got[-1][1]
    near = [(0, weight)]
    for j, w in mine[1:]:
        if split:
            other = swap(w, "rep", n_rep, 0)
            whole = jnp.zeros_like(weight)
            whole = lax.dynamic_update_slice_in_dim(whole, w, lane * half, axis=0)
            w = lax.dynamic_update_slice_in_dim(whole, other, (1 - lane) * half, axis=0)
        near.append((j, w))
    pieces = []
    for j, w in near:
        pieces.append(((me ^ j) * rows, w))
        if n_shard > 1:
            pieces.append(((me ^ j ^ 1) * rows, swap(w, "shard", n_shard, 0)))
    return pieces, earlier


def times(left, pieces):
    total = None
    for start, w in pieces:
        part = matmul(lax.dynamic_slice_in_dim(left, start, w.shape[0], axis=1), w)
        total = part if total is None else total + part
    return total


def times_t(left, pieces, depth):
    total = jnp.zeros((left.shape[0], depth), jnp.float32)
    for start, w in pieces:
        part = lax.dot_general(left, w, (((1,), (1,)), ((), ())), preferred_element_type=jnp.float32)
        total = lax.dynamic_update_slice_in_dim(total, part, start, axis=1)
    return total


def relative_rows(left, n_shard, n_rep):
    tok, depth = left.shape
    s_bits, r_bits = bit_count(n_shard), bit_count(n_rep)
    rows = depth // (n_shard * n_rep)
    blocks = left.T.reshape((2,) * (s_bits + r_bits) + (rows, tok))
    order = tuple(reversed(range(s_bits))) + tuple(reversed(range(s_bits, s_bits + r_bits)))
    blocks = blocks.transpose(order + (s_bits + r_bits, s_bits + r_bits + 1))
    me, rep = lax.axis_index("shard"), lax.axis_index("rep")
    for i in range(s_bits + r_bits):
        on = ((me >> i) & 1) if i < s_bits else ((rep >> (i - s_bits)) & 1)
        blocks = jnp.where(on == 1, jnp.flip(blocks, axis=i), blocks)
    return blocks


def grad_of(blocks, right, n_shard, n_rep, latest):
    s_bits, r_bits = bit_count(n_shard), bit_count(n_rep)
    cols = right.shape[1]

    def part(rows_of):
        return matmul(rows_of.reshape(-1, rows_of.shape[-1]), right).astype(jnp.bfloat16)

    steps = [("shard", n_shard, i) for i in range(s_bits)] + [("rep", n_rep, i) for i in range(r_bits)]
    if not steps:
        return part(blocks).astype(jnp.float32)
    send, keep = part(blocks[1]), part(blocks[0])
    for k, (name, size, bit) in enumerate(steps):
        if name == "shard" and bit > 0:
            send = after(send, latest.get(bit))
        got = swap(send, name, size, bit)
        if name == "shard" and bit > 0:
            latest[bit] = got
        total = (keep.astype(jnp.float32) + got.astype(jnp.float32)).astype(jnp.bfloat16)
        if k + 1 < len(steps):
            half = total.shape[0] // 2
            keep, send = total[:half], total[half:]
    return lax.all_gather(total, "rep", axis=0, tiled=True).astype(jnp.float32)


def local(
    n_rep,
    n_shard,
    tokens,
    cotangent,
    doc_ids,
    w_query,
    w_key,
    w_value,
    w_out,
    w_gate,
    w_up,
    w_down,
    gain_attn,
    gain_ffn,
    gain_query,
    gain_key,
):
    tok_rows, width = tokens.shape
    ff = w_gate.shape[1]
    q_width, k_width = w_query.shape[1], w_key.shape[1]
    head_share = QH // KVH
    score_scale = 1.0 / math.sqrt(HEAD_DIM)
    gains = (gain_attn, gain_ffn, gain_query, gain_key)
    gain_sizes = [g.shape[0] for g in gains]
    gain_ends = [sum(gain_sizes[: i + 1]) for i in range(len(gains))]
    all_gains = gather_small(jnp.concatenate(gains), n_shard)
    latest = {}
    full_gattn, full_gffn, full_gquery, full_gkey = (
        all_gains[:, end - size : end].reshape(-1) for size, end in zip(gain_sizes, gain_ends)
    )
    w_qkv = jnp.concatenate([w_query, w_key, w_value], axis=1)
    qkv_set, last = gather_pieces(w_qkv, n_shard, n_rep, all_gains)
    out_set, last = gather_pieces(w_out, n_shard, n_rep, last)
    gate_set, last = gather_pieces(w_gate, n_shard, n_rep, last)
    up_set, last = gather_pieces(w_up, n_shard, n_rep, last)
    down_set, last = gather_pieces(w_down, n_shard, n_rep, last)

    doc_rows = doc_ids[None, :]
    allowed, positions = doc_tables(doc_rows)
    key_mask = allowed[:, None, None]
    cos_tab, sin_tab = rope_tables(positions, HEAD_DIM)
    resid_in = tokens.astype(jnp.float32)
    normed_in, unit_in, rms_in = norm_rows(resid_in, full_gattn)
    normed_bf = normed_in.astype(jnp.bfloat16)
    qkv = times(normed_bf, qkv_set)
    query_raw = qkv[:, :q_width].reshape(1, tok_rows, QH, HEAD_DIM)
    key_raw = qkv[:, q_width : q_width + k_width].reshape(1, tok_rows, KVH, HEAD_DIM)
    value_bf = qkv[:, q_width + k_width :].astype(jnp.bfloat16).reshape(1, tok_rows, KVH, HEAD_DIM)
    query_normed, query_unit, query_rms = norm_rows(query_raw, full_gquery)
    key_normed, key_unit, key_rms = norm_rows(key_raw, full_gkey)
    query_bf = (
        rotate(query_normed, cos_tab, sin_tab)
        .astype(jnp.bfloat16)
        .reshape(1, tok_rows, KVH, head_share, HEAD_DIM)
    )
    key_bf = rotate(key_normed, cos_tab, sin_tab).astype(jnp.bfloat16)
    attn_probs, log_total = attn_probs_of(query_bf, key_bf, key_mask, None, score_scale)
    probs_bf = attn_probs.astype(jnp.bfloat16)
    mixed_bf = (
        jnp.einsum("gkrqs,gskd->gqkrd", probs_bf, value_bf, preferred_element_type=jnp.float32)
        .astype(jnp.bfloat16)
        .reshape(tok_rows, QH * HEAD_DIM)
    )
    resid_mid = resid_in + times(mixed_bf, out_set)
    normed_mid, unit_mid, rms_mid = norm_rows(resid_mid, full_gffn)
    hidden_in = normed_mid.astype(jnp.bfloat16)
    gate_proj = times(hidden_in, gate_set)
    up_proj = times(hidden_in, up_set)
    gate_sig = jax.nn.sigmoid(gate_proj)
    gate_act = gate_proj * gate_sig
    hidden_bf = (gate_act * up_proj).astype(jnp.bfloat16)

    live_rows = (doc_ids >= 0).astype(jnp.float32)[:, None]
    grad_y = cotangent.astype(jnp.float32) * live_rows
    grad_y_bf = grad_y.astype(jnp.bfloat16)
    grad_down = grad_of(relative_rows(hidden_bf, n_shard, n_rep), grad_y_bf, n_shard, n_rep, latest)
    block_out = (resid_mid + times(hidden_bf, down_set)).astype(jnp.bfloat16)

    grad_hidden = times_t(grad_y_bf, down_set, ff)
    grad_gate_bf = (grad_hidden * up_proj * gate_sig * (1.0 + gate_proj * (1.0 - gate_sig))).astype(
        jnp.bfloat16
    )
    grad_up_bf = (grad_hidden * gate_act).astype(jnp.bfloat16)
    mid_rows = relative_rows(hidden_in, n_shard, n_rep)
    grad_gate = grad_of(mid_rows, grad_gate_bf, n_shard, n_rep, latest)
    grad_up = grad_of(mid_rows, grad_up_bf, n_shard, n_rep, latest)
    grad_norm_mid = times_t(grad_gate_bf, gate_set, width) + times_t(grad_up_bf, up_set, width)
    back_mid, part_gffn = norm_back(grad_norm_mid, unit_mid, rms_mid, full_gffn)
    grad_mid = grad_y + back_mid
    grad_mid_bf = grad_mid.astype(jnp.bfloat16)
    grad_out = grad_of(relative_rows(mixed_bf, n_shard, n_rep), grad_mid_bf, n_shard, n_rep, latest)
    grad_mixed_bf = (
        times_t(grad_mid_bf, out_set, q_width)
        .astype(jnp.bfloat16)
        .reshape(1, tok_rows, KVH, head_share, HEAD_DIM)
    )
    grad_scores = jnp.einsum(
        "gqkrd,gskd->gkrqs", grad_mixed_bf, value_bf, preferred_element_type=jnp.float32
    )
    grad_value_bf = (
        jnp.einsum("gkrqs,gqkrd->gskd", probs_bf, grad_mixed_bf, preferred_element_type=jnp.float32)
        .astype(jnp.bfloat16)
        .reshape(tok_rows, KVH * HEAD_DIM)
    )
    row_dot = jnp.sum(attn_probs * grad_scores, axis=-1, keepdims=True)
    grad_logits = (attn_probs * (grad_scores - row_dot) * score_scale).astype(jnp.bfloat16)
    grad_query_rot = jnp.einsum(
        "gkrqs,gskd->gqkrd", grad_logits, key_bf, preferred_element_type=jnp.float32
    ).reshape(1, tok_rows, QH, HEAD_DIM)
    grad_key_rot = jnp.einsum(
        "gkrqs,gqkrd->gskd", grad_logits, query_bf, preferred_element_type=jnp.float32
    )
    grad_query_raw, part_gquery = norm_back(
        rotate_back(grad_query_rot, cos_tab, sin_tab), query_unit, query_rms, full_gquery
    )
    grad_key_raw, part_gkey = norm_back(
        rotate_back(grad_key_rot, cos_tab, sin_tab), key_unit, key_rms, full_gkey
    )
    grad_query_bf = grad_query_raw.astype(jnp.bfloat16).reshape(tok_rows, QH * HEAD_DIM)
    grad_key_bf = grad_key_raw.astype(jnp.bfloat16).reshape(tok_rows, KVH * HEAD_DIM)
    grad_qkv_bf = jnp.concatenate([grad_query_bf, grad_key_bf, grad_value_bf], axis=1)
    grad_qkv = grad_of(relative_rows(normed_bf, n_shard, n_rep), grad_qkv_bf, n_shard, n_rep, latest)
    grad_query = grad_qkv[:, :q_width]
    grad_key = grad_qkv[:, q_width : q_width + k_width]
    grad_value = grad_qkv[:, q_width + k_width :]
    grad_norm_in = times_t(grad_qkv_bf, qkv_set, width)
    back_in, part_gattn = norm_back(grad_norm_in, unit_in, rms_in, full_gattn)
    grad_tokens = grad_mid + back_in
    part_gains = jnp.concatenate(
        [
            p.reshape(n_shard, -1)
            for p in (part_gattn, part_gffn, part_gquery, part_gkey)
        ],
        axis=1,
    )
    part_gains = part_gains.astype(jnp.bfloat16).astype(jnp.float32)
    sum_gains = part_gains
    for name, size in (("shard", n_shard), ("rep", n_rep)):
        for bit in range(bit_count(size)):
            sum_gains = sum_gains + swap(sum_gains, name, size, bit)
    own_gains = lax.dynamic_index_in_dim(sum_gains, lax.axis_index("shard"), axis=0, keepdims=False)
    grad_gattn, grad_gffn, grad_gquery, grad_gkey = (
        own_gains[end - size : end] for size, end in zip(gain_sizes, gain_ends)
    )
    return (
        block_out,
        grad_tokens,
        grad_query,
        grad_key,
        grad_value,
        grad_out,
        grad_gate,
        grad_up,
        grad_down,
        grad_gattn,
        grad_gffn,
        grad_gquery,
        grad_gkey,
    )


def solution(mesh):
    return jax.shard_map(
        functools.partial(local, mesh.shape["rep"], mesh.shape["shard"]),
        mesh=mesh,
        in_specs=(
            P(("rep", "shard"), None),
            P(("rep", "shard"), None),
            P(("rep", "shard")),
            P("shard", None),
            P("shard", None),
            P("shard", None),
            P("shard", None),
            P("shard", None),
            P("shard", None),
            P("shard", None),
            P("shard"),
            P("shard"),
            P("shard"),
            P("shard"),
        ),
        out_specs=(
            P(("rep", "shard"), None),
            P(("rep", "shard"), None),
            P("shard", None),
            P("shard", None),
            P("shard", None),
            P("shard", None),
            P("shard", None),
            P("shard", None),
            P("shard", None),
            P("shard"),
            P("shard"),
            P("shard"),
            P("shard"),
        ),
        check_vma=False,
    )
```

```python
import functools
import math

import jax
import jax.numpy as jnp
from jax import lax
from jax.sharding import PartitionSpec as P

QH = 16
KVH = 8
HEAD_DIM = 64


NORM_EPSILON = 1e-05
ROPE_BASE = 1000000.0


def matmul(left, right):
    return jnp.dot(left, right, preferred_element_type=jnp.float32)


def norm_rows(values, gain_vec):
    inv_rms = lax.rsqrt(jnp.mean(values * values, axis=-1, keepdims=True) + NORM_EPSILON)
    normed = values * inv_rms
    return (normed * gain_vec.astype(jnp.float32), normed, inv_rms)


def norm_back(grad_out, normed, inv_rms, gain_vec):
    scaled = grad_out * gain_vec.astype(jnp.float32)
    grad_in = inv_rms * (scaled - normed * jnp.mean(scaled * normed, axis=-1, keepdims=True))
    lead_axes = tuple(range(grad_out.ndim - 1))
    return (grad_in, jnp.sum(grad_out * normed, axis=lead_axes))


def doc_tables(doc_rows):
    block_len = doc_rows.shape[-1]
    row_index = jnp.arange(block_len)[:, None]
    col_index = jnp.arange(block_len)[None, :]
    same_doc = doc_rows[:, :, None] == doc_rows[:, None, :]
    allowed = same_doc & (row_index >= col_index)[None]
    earlier = same_doc & (row_index > col_index)[None]
    positions = jnp.sum(earlier.astype(jnp.int32), axis=2)
    return (allowed, positions)


def rope_tables(positions, head_dim):
    half_dim = head_dim // 2
    inv_freq = jnp.exp(
        jnp.arange(half_dim).astype(jnp.float32) * (-2.0 * math.log(ROPE_BASE) / head_dim)
    )
    angles = positions.astype(jnp.float32)[:, :, None, None] * inv_freq
    return (jnp.cos(angles), jnp.sin(angles))


def rotate(values, cos_tab, sin_tab):
    half_dim = values.shape[-1] // 2
    part_one = values[..., :half_dim]
    part_two = values[..., half_dim:]
    return jnp.concatenate(
        [part_one * cos_tab - part_two * sin_tab, part_two * cos_tab + part_one * sin_tab], axis=-1
    )


def rotate_back(values, cos_tab, sin_tab):
    half_dim = values.shape[-1] // 2
    part_one = values[..., :half_dim]
    part_two = values[..., half_dim:]
    return jnp.concatenate(
        [part_one * cos_tab + part_two * sin_tab, part_two * cos_tab - part_one * sin_tab], axis=-1
    )


def attn_probs_of(query_bf, key_bf, key_mask, log_total, score_scale):
    scores = (
        jnp.einsum("gqkrd,gskd->gkrqs", query_bf, key_bf, preferred_element_type=jnp.float32)
        * score_scale
    )
    if log_total is None:
        log_total = jnp.log(
            jnp.sum(jnp.where(key_mask, jnp.exp(scores), 0.0), axis=-1, keepdims=True)
        )
    return (jnp.where(key_mask, jnp.exp(scores - log_total), 0.0), log_total)


def bit_count(size):
    return size.bit_length() - 1


def swap(values, axis_name, axis_size, bit):
    return lax.ppermute(values, axis_name, [(i, i ^ (1 << bit)) for i in range(axis_size)])


def after(values, earlier):
    if earlier is None:
        return values
    return lax.optimization_barrier((values, earlier))[0]


def gather_small(values, n_shard):
    rows = [values] + [
        lax.ppermute(values, "shard", [(i, i ^ j) for i in range(n_shard)]) for j in range(1, n_shard)
    ]
    got = jnp.stack(rows)
    me = lax.axis_index("shard")
    for bit in range(bit_count(n_shard)):
        pairs = got.reshape(-1, 2, 1 << bit, got.shape[-1])
        got = jnp.where((me >> bit) & 1 == 1, jnp.flip(pairs, axis=1), pairs).reshape(got.shape)
    return got


def gather_pieces(weight, n_shard, n_rep, earlier):
    rows = weight.shape[0]
    me = lax.axis_index("shard")
    split = n_rep > 1 and rows % 2 == 0
    first = weight
    if split:
        half = rows // 2
        lane = lax.axis_index("rep") & 1
        first = lax.dynamic_slice_in_dim(weight, lane * half, half, axis=0)
    mine = [(0, first)]
    for bit in reversed(range(1, bit_count(n_shard))):
        sent = [(j, after(w, earlier)) for j, w in mine]
        got = [(j ^ (1 << bit), swap(w, "shard", n_shard, bit)) for j, w in sent]
        mine, earlier = mine + got, got[-1][1]
    near = [(0, weight)]
    for j, w in mine[1:]:
        if split:
            other = swap(w, "rep", n_rep, 0)
            whole = jnp.zeros_like(weight)
            whole = lax.dynamic_update_slice_in_dim(whole, w, lane * half, axis=0)
            w = lax.dynamic_update_slice_in_dim(whole, other, (1 - lane) * half, axis=0)
        near.append((j, w))
    pieces = []
    for j, w in near:
        pieces.append(((me ^ j) * rows, w))
        if n_shard > 1:
            pieces.append(((me ^ j ^ 1) * rows, swap(w, "shard", n_shard, 0)))
    return pieces, earlier


def times(left, pieces):
    total = None
    for start, w in pieces:
        part = matmul(lax.dynamic_slice_in_dim(left, start, w.shape[0], axis=1), w)
        total = part if total is None else total + part
    return total


def times_t(left, pieces, depth):
    total = jnp.zeros((left.shape[0], depth), jnp.float32)
    for start, w in pieces:
        part = lax.dot_general(left, w, (((1,), (1,)), ((), ())), preferred_element_type=jnp.float32)
        total = lax.dynamic_update_slice_in_dim(total, part, start, axis=1)
    return total


def relative_rows(left, n_shard, n_rep):
    tok, depth = left.shape
    s_bits, r_bits = bit_count(n_shard), bit_count(n_rep)
    rows = depth // (n_shard * n_rep)
    blocks = left.T.reshape((2,) * (s_bits + r_bits) + (rows, tok))
    order = tuple(reversed(range(s_bits))) + tuple(reversed(range(s_bits, s_bits + r_bits)))
    blocks = blocks.transpose(order + (s_bits + r_bits, s_bits + r_bits + 1))
    me, rep = lax.axis_index("shard"), lax.axis_index("rep")
    for i in range(s_bits + r_bits):
        on = ((me >> i) & 1) if i < s_bits else ((rep >> (i - s_bits)) & 1)
        blocks = jnp.where(on == 1, jnp.flip(blocks, axis=i), blocks)
    return blocks


def near_sum(blocks, right, n_shard):
    def part(rows_of):
        return matmul(rows_of.reshape(-1, rows_of.shape[-1]), right).astype(jnp.bfloat16)

    send, keep = part(blocks[1]), part(blocks[0])
    return join(keep, swap(send, "shard", n_shard, 0))


def join(keep, got):
    return (keep.astype(jnp.float32) + got.astype(jnp.float32)).astype(jnp.bfloat16)


def far_sum(total, n_shard, n_rep, latest):
    steps = [("shard", n_shard, i) for i in range(1, bit_count(n_shard))]
    steps += [("rep", n_rep, i) for i in range(bit_count(n_rep))]
    for name, size, bit in steps:
        half = total.shape[0] // 2
        keep, send = total[:half], total[half:]
        if name == "shard":
            send = after(send, latest.get(bit))
        got = swap(send, name, size, bit)
        if name == "shard":
            latest[bit] = got
        total = join(keep, got)
    return total


def rep_gather(rows, n_rep, by_swaps):
    if not by_swaps:
        return lax.all_gather(rows, "rep", axis=0, tiled=True).astype(jnp.float32)
    cols = rows.shape[-1]
    rep = lax.axis_index("rep")
    for bit in reversed(range(bit_count(n_rep))):
        got = swap(rows, "rep", n_rep, bit)
        axis = rows.ndim - 2
        rows = jnp.where(
            (rep >> bit) & 1 == 1,
            jnp.stack([got, rows], axis=axis),
            jnp.stack([rows, got], axis=axis),
        )
    return rows.reshape(-1, cols).astype(jnp.float32)


def local(
    n_rep,
    n_shard,
    tokens,
    cotangent,
    doc_ids,
    w_query,
    w_key,
    w_value,
    w_out,
    w_gate,
    w_up,
    w_down,
    gain_attn,
    gain_ffn,
    gain_query,
    gain_key,
):
    tok_rows, width = tokens.shape
    ff = w_gate.shape[1]
    q_width, k_width = w_query.shape[1], w_key.shape[1]
    head_share = QH // KVH
    score_scale = 1.0 / math.sqrt(HEAD_DIM)
    gains = (gain_attn, gain_ffn, gain_query, gain_key)
    gain_sizes = [g.shape[0] for g in gains]
    gain_ends = [sum(gain_sizes[: i + 1]) for i in range(len(gains))]
    all_gains = gather_small(jnp.concatenate(gains), n_shard)
    latest = {}
    full_gattn, full_gffn, full_gquery, full_gkey = (
        all_gains[:, end - size : end].reshape(-1) for size, end in zip(gain_sizes, gain_ends)
    )
    w_qkv = jnp.concatenate([w_query, w_key, w_value], axis=1)
    qkv_set, last = gather_pieces(w_qkv, n_shard, n_rep, all_gains)
    out_set, last = gather_pieces(w_out, n_shard, n_rep, last)
    gate_set, last = gather_pieces(w_gate, n_shard, n_rep, last)
    up_set, last = gather_pieces(w_up, n_shard, n_rep, last)
    down_set, last = gather_pieces(w_down, n_shard, n_rep, last)

    doc_rows = doc_ids[None, :]
    allowed, positions = doc_tables(doc_rows)
    key_mask = allowed[:, None, None]
    cos_tab, sin_tab = rope_tables(positions, HEAD_DIM)
    resid_in = tokens.astype(jnp.float32)
    normed_in, unit_in, rms_in = norm_rows(resid_in, full_gattn)
    normed_bf = normed_in.astype(jnp.bfloat16)
    qkv = times(normed_bf, qkv_set)
    query_raw = qkv[:, :q_width].reshape(1, tok_rows, QH, HEAD_DIM)
    key_raw = qkv[:, q_width : q_width + k_width].reshape(1, tok_rows, KVH, HEAD_DIM)
    value_bf = qkv[:, q_width + k_width :].astype(jnp.bfloat16).reshape(1, tok_rows, KVH, HEAD_DIM)
    query_normed, query_unit, query_rms = norm_rows(query_raw, full_gquery)
    key_normed, key_unit, key_rms = norm_rows(key_raw, full_gkey)
    query_bf = (
        rotate(query_normed, cos_tab, sin_tab)
        .astype(jnp.bfloat16)
        .reshape(1, tok_rows, KVH, head_share, HEAD_DIM)
    )
    key_bf = rotate(key_normed, cos_tab, sin_tab).astype(jnp.bfloat16)
    attn_probs, log_total = attn_probs_of(query_bf, key_bf, key_mask, None, score_scale)
    probs_bf = attn_probs.astype(jnp.bfloat16)
    mixed_bf = (
        jnp.einsum("gkrqs,gskd->gqkrd", probs_bf, value_bf, preferred_element_type=jnp.float32)
        .astype(jnp.bfloat16)
        .reshape(tok_rows, QH * HEAD_DIM)
    )
    resid_mid = resid_in + times(mixed_bf, out_set)
    normed_mid, unit_mid, rms_mid = norm_rows(resid_mid, full_gffn)
    hidden_in = normed_mid.astype(jnp.bfloat16)
    gate_proj = times(hidden_in, gate_set)
    up_proj = times(hidden_in, up_set)
    gate_sig = jax.nn.sigmoid(gate_proj)
    gate_act = gate_proj * gate_sig
    hidden_bf = (gate_act * up_proj).astype(jnp.bfloat16)

    live_rows = (doc_ids >= 0).astype(jnp.float32)[:, None]
    grad_y = cotangent.astype(jnp.float32) * live_rows
    grad_y_bf = grad_y.astype(jnp.bfloat16)
    near_down = near_sum(relative_rows(hidden_bf, n_shard, n_rep), grad_y_bf, n_shard)
    block_out = (resid_mid + times(hidden_bf, down_set)).astype(jnp.bfloat16)

    grad_hidden = times_t(grad_y_bf, down_set, ff)
    grad_gate_bf = (grad_hidden * up_proj * gate_sig * (1.0 + gate_proj * (1.0 - gate_sig))).astype(
        jnp.bfloat16
    )
    grad_up_bf = (grad_hidden * gate_act).astype(jnp.bfloat16)
    mid_rows = relative_rows(hidden_in, n_shard, n_rep)
    near_gate = near_sum(mid_rows, grad_gate_bf, n_shard)
    near_up = near_sum(mid_rows, grad_up_bf, n_shard)
    near_down, gate_in = lax.optimization_barrier((near_down, grad_gate_bf))
    own_down = far_sum(near_down, n_shard, n_rep, latest)
    got_down = list(latest.values())
    near_gate, near_up = lax.optimization_barrier((near_gate, near_up))
    own_gate = far_sum(near_gate, n_shard, n_rep, latest)
    got_gate = list(latest.values())
    own_up = far_sum(near_up, n_shard, n_rep, latest)
    grad_down = rep_gather(own_down, n_rep, False)
    grad_gate = rep_gather(own_gate, n_rep, False)
    grad_up = rep_gather(own_up, n_rep, True)
    grad_norm_mid = times_t(gate_in, gate_set, width) + times_t(grad_up_bf, up_set, width)
    back_mid, part_gffn = norm_back(grad_norm_mid, unit_mid, rms_mid, full_gffn)
    grad_mid = grad_y + back_mid
    grad_mid_bf = after(grad_mid.astype(jnp.bfloat16), got_down)
    near_out = near_sum(relative_rows(mixed_bf, n_shard, n_rep), grad_mid_bf, n_shard)
    grad_mixed_bf = (
        times_t(grad_mid_bf, out_set, q_width)
        .astype(jnp.bfloat16)
        .reshape(1, tok_rows, KVH, head_share, HEAD_DIM)
    )
    grad_scores = jnp.einsum(
        "gqkrd,gskd->gkrqs", grad_mixed_bf, value_bf, preferred_element_type=jnp.float32
    )
    grad_value_bf = (
        jnp.einsum("gkrqs,gqkrd->gskd", probs_bf, grad_mixed_bf, preferred_element_type=jnp.float32)
        .astype(jnp.bfloat16)
        .reshape(tok_rows, KVH * HEAD_DIM)
    )
    row_dot = jnp.sum(attn_probs * grad_scores, axis=-1, keepdims=True)
    grad_logits = (attn_probs * (grad_scores - row_dot) * score_scale).astype(jnp.bfloat16)
    grad_logits = after(grad_logits, got_gate)
    grad_query_rot = jnp.einsum(
        "gkrqs,gskd->gqkrd", grad_logits, key_bf, preferred_element_type=jnp.float32
    ).reshape(1, tok_rows, QH, HEAD_DIM)
    grad_key_rot = jnp.einsum(
        "gkrqs,gqkrd->gskd", grad_logits, query_bf, preferred_element_type=jnp.float32
    )
    grad_query_raw, part_gquery = norm_back(
        rotate_back(grad_query_rot, cos_tab, sin_tab), query_unit, query_rms, full_gquery
    )
    grad_key_raw, part_gkey = norm_back(
        rotate_back(grad_key_rot, cos_tab, sin_tab), key_unit, key_rms, full_gkey
    )
    grad_query_bf = grad_query_raw.astype(jnp.bfloat16).reshape(tok_rows, QH * HEAD_DIM)
    grad_key_bf = grad_key_raw.astype(jnp.bfloat16).reshape(tok_rows, KVH * HEAD_DIM)
    grad_qkv_bf = jnp.concatenate([grad_query_bf, grad_key_bf, grad_value_bf], axis=1)
    near_qkv = near_sum(relative_rows(normed_bf, n_shard, n_rep), grad_qkv_bf, n_shard)
    near_attn = jnp.concatenate([near_qkv, near_out], axis=1)
    grad_attn = rep_gather(far_sum(near_attn, n_shard, n_rep, latest), n_rep, True)
    ends = [q_width, q_width + k_width, q_width + 2 * k_width]
    grad_query, grad_key, grad_value, grad_out = jnp.split(grad_attn, ends, axis=1)
    grad_norm_in = times_t(grad_qkv_bf, qkv_set, width)
    back_in, part_gattn = norm_back(grad_norm_in, unit_in, rms_in, full_gattn)
    grad_tokens = grad_mid + back_in
    part_gains = jnp.concatenate(
        [
            p.reshape(n_shard, -1)
            for p in (part_gattn, part_gffn, part_gquery, part_gkey)
        ],
        axis=1,
    )
    part_gains = part_gains.astype(jnp.bfloat16).astype(jnp.float32)
    sum_gains = part_gains
    for name, size in (("shard", n_shard), ("rep", n_rep)):
        for bit in range(bit_count(size)):
            sum_gains = sum_gains + swap(sum_gains, name, size, bit)
    own_gains = lax.dynamic_index_in_dim(sum_gains, lax.axis_index("shard"), axis=0, keepdims=False)
    grad_gattn, grad_gffn, grad_gquery, grad_gkey = (
        own_gains[end - size : end] for size, end in zip(gain_sizes, gain_ends)
    )
    return (
        block_out,
        grad_tokens,
        grad_query,
        grad_key,
        grad_value,
        grad_out,
        grad_gate,
        grad_up,
        grad_down,
        grad_gattn,
        grad_gffn,
        grad_gquery,
        grad_gkey,
    )


def solution(mesh):
    return jax.shard_map(
        functools.partial(local, mesh.shape["rep"], mesh.shape["shard"]),
        mesh=mesh,
        in_specs=(
            P(("rep", "shard"), None),
            P(("rep", "shard"), None),
            P(("rep", "shard")),
            P("shard", None),
            P("shard", None),
            P("shard", None),
            P("shard", None),
            P("shard", None),
            P("shard", None),
            P("shard", None),
            P("shard"),
            P("shard"),
            P("shard"),
            P("shard"),
        ),
        out_specs=(
            P(("rep", "shard"), None),
            P(("rep", "shard"), None),
            P("shard", None),
            P("shard", None),
            P("shard", None),
            P("shard", None),
            P("shard", None),
            P("shard", None),
            P("shard", None),
            P("shard"),
            P("shard"),
            P("shard"),
            P("shard"),
        ),
        check_vma=False,
    )
```
